256 devices in a mesh: chan: 16 (over y, x_lo, core), stn: 16 (over z, x_hi).
Axes of the slice: x: 4 (x_hi: 2, x_lo: 2; x = x_hi * 2 + x_lo), y: 4, z: 8, core: 2. Of those that a mesh axis runs over, the one named last changes fastest.
Arguments:
- voltages: bfloat16 [1024, 196608], P('stn', 'chan'), may hold values from -6 to 6
- pfb_taps: float32 [16, 512], replicated, may hold values from -1.5 to 1.5
- flags: int32 [512, 256, 48], P('stn', 'chan'), may hold values 0 or 1
Outputs:
- visibilities: float32 [256, 2, 1024, 1024], P('chan', None, 'stn')
The draws below stay inside these ranges and needn't reach their ends.
All inputs are finite; a program needn't handle non-finite values. No bound on the sum of `flags` on one device may be relied on, other than what follows from the above.
Results may differ from the reference program's by a relative error of at most 0.0062.
Values may be sent and summed in bfloat16 or wider, within the bound.
A program may use at most 128 MiB of HBM per device.

```python
import math
import jax
import jax.numpy as jnp
from jax import lax

STATIONS = 512
POLS = 2
CHANNELS = 256
TAPS = 16
FBLK = 8
SIGNALS = 1024
NFFT = 512
SPECTRA = 384
FBLOCKS = 48


def plant(result, stream_key, smallest, top_value):
    spot = [jax.random.randint(jax.random.fold_in(stream_key, axis), (), 0, length) for axis, length in enumerate(result.shape)]
    widest = result.shape.index(max(result.shape))
    next_to = spot[:widest] + [(spot[widest] + 1) % result.shape[widest]] + spot[widest + 1:]
    return result.at[tuple(spot)].set(smallest).at[tuple(next_to)].set(top_value)


def level_of(rng, dims, cuts, smallest, top_value):
    loudness = 1.0
    for axis_at, blocks in cuts:
        heights = jax.random.uniform(jax.random.fold_in(jax.random.fold_in(rng, 6), axis_at), (blocks,), jnp.float32, smallest / len(cuts), top_value / len(cuts))
        loudness = loudness * jnp.repeat(jnp.exp(heights), dims[axis_at] // blocks).reshape((-1,) + (1,) * (len(dims) - 1 - axis_at))
    return loudness


def noise(key, dims, scale, limit, cuts=(), kind=jnp.bfloat16):
    values = jax.random.normal(key, dims, jnp.float32) * scale
    if len(cuts) > 0:
        values = level_of(key, dims, cuts, -0.22, 0.18) * values
    return jnp.clip(values, min=-limit, max=limit).astype(kind)


def setup_inputs(seed: int = 0) -> dict:
    streams_of = jax.random.split(jax.random.key(seed), 4)
    return {
        "voltages": noise(streams_of[0], (SIGNALS, SPECTRA * NFFT), 1.0, 6.0, ((0, 16), (1, 16))),
        "pfb_taps": noise(streams_of[1], (TAPS, NFFT), 0.25, 1.5, (), jnp.float32),
        "flags": plant((jax.random.randint(streams_of[2], (STATIONS, CHANNELS, FBLOCKS), 0, 4) < 3).astype(jnp.int32), jax.random.fold_in(streams_of[2], 1), 0, 1),
    }


def dft_table(length):
    rows_index = jnp.arange(length, dtype=jnp.int32)
    chan_index = rows_index // 2
    sample_index = jnp.arange(length, dtype=jnp.int32)
    phase_step = chan_index[:, None] * sample_index[None, :] % length
    angles = phase_step.astype(jnp.float32) * (2.0 * math.pi / length)
    values = jnp.where((rows_index % 2 == 0)[:, None], jnp.cos(angles), -jnp.sin(angles))
    return (values / math.sqrt(length)).astype(jnp.bfloat16)

def reference(voltages, pfb_taps, flags):
    frames = voltages.reshape(SIGNALS, SPECTRA, NFFT)
    padded = jnp.pad(frames, ((0, 0), (TAPS - 1, 0), (0, 0)))
    filtered = jnp.zeros((SIGNALS, SPECTRA, NFFT), jnp.float32)
    for tap_index in range(TAPS):
        offset = TAPS - 1 - tap_index
        filtered = filtered + pfb_taps[tap_index] * padded[:, offset:offset + SPECTRA, :].astype(jnp.float32)
    filtered = filtered.astype(jnp.bfloat16)
    table = dft_table(NFFT)
    spectra = jnp.einsum('qn,stn->qst', table.astype(jnp.float32), filtered.astype(jnp.float32)).astype(jnp.bfloat16)
    keep = jnp.transpose(flags, (1, 0, 2)).astype(jnp.bfloat16)[:, None, :, None, :, None]
    weighted = (spectra.reshape(CHANNELS, 2, STATIONS, POLS, FBLOCKS, FBLK) * keep).reshape(CHANNELS, 2, SIGNALS, SPECTRA)

    def one_channel(block):
        block = block.astype(jnp.float32)
        prods = jnp.einsum('pat,qbt->pqab', block, block)
        real_part = prods[0, 0] + prods[1, 1]
        imag_part = prods[1, 0] - prods[0, 1]
        return jnp.stack([real_part, imag_part], axis=0) / float(SPECTRA)
    return lax.map(one_channel, weighted)
```

```python
import functools
import math

import jax
import jax.numpy as jnp
import ml_dtypes
import numpy as np
from jax import lax
from jax.experimental import pallas as pl
from jax.experimental.pallas import tpu as pltpu
from jax.sharding import PartitionSpec as P

POLS = 2
BF16 = jnp.bfloat16
F32 = jnp.float32
MESH = pl.DeviceIdType.MESH


def dft_table(length, chans, stns):
    sample = np.arange(length)
    order = np.arange(length // 2).reshape(chans, stns).T.reshape(-1)
    phase = (order[:, None] * sample[None, :]) % length
    angles = phase.astype(np.float32) * np.float32(2.0 * math.pi / length)
    angles = angles.astype(np.float64)
    values = np.concatenate([np.cos(angles), -np.sin(angles)], axis=0)
    return (values.astype(np.float32) / np.float32(math.sqrt(length))).astype(ml_dtypes.bfloat16)


def spread(stations, blocks, lanes):
    out = np.zeros((blocks, lanes, lanes), np.float32)
    for fb in range(blocks):
        for lane in range(lanes):
            out[fb, fb * stations + (lane % (lanes // 2)) // POLS, lane] = 1.0
    return out.astype(ml_dtypes.bfloat16)


def kernel(
    n,
    v_ref, taps_ref, tab_ref, mask_ref, spread_ref,
    o_ref,
    ext, filt, w32, wb, rz, bb, mk, mx, zy, zt, sb,
    vsem, hsend, hrecv, msend, mrecv, zsend, zrecv, csend, crecv, osend, orecv, lsem,
):
    ci = lax.axis_index("chan")
    sk = lax.axis_index("stn")
    nfft = 512
    halo = 15
    own = v_ref.shape[1] // nfft

    def stn_at(d):
        return lax.rem(sk + d, n)

    def chan_at(d):
        return lax.rem(ci + d, n)

    load = pltpu.make_async_copy(v_ref, ext.at[:, halo * nfft :], vsem)
    load.start()

    bar = pltpu.get_barrier_semaphore()

    @pl.loop(1, n)
    def _(d):
        pl.semaphore_signal(bar, inc=1, device_id={"stn": stn_at(d)}, device_id_type=MESH)
        pl.semaphore_signal(bar, inc=1, device_id={"chan": chan_at(d)}, device_id_type=MESH)

    def fir(fb):
        @pl.loop(0, 16)
        def _(idx):
            s0 = pl.multiple_of((idx // 4) * 16, 16)
            n0 = pl.multiple_of(lax.rem(idx, 4) * 128, 128)
            taps = [taps_ref[pl.ds(k, 1), pl.ds(n0, 128)] for k in range(16)]
            x = [
                ext[pl.ds(s0, 16), pl.ds(pl.multiple_of((fb * 8 + f) * nfft + n0, 128), 128)].astype(F32)
                for f in range(23)
            ]
            for t in range(8):
                acc = taps[0] * x[t + 15]
                for k in range(1, 16):
                    acc = acc + taps[k] * x[t + 15 - k]
                filt[pl.ds(pl.multiple_of(t * 64 + s0, 16), 16), pl.ds(n0, 128)] = acc.astype(BF16)

    def dft(fb):
        for tt in range(2):
            for p in range(2):
                o = lax.dot_general(
                    tab_ref[p * 256 : (p + 1) * 256, :], filt[tt * 256 : (tt + 1) * 256, :],
                    (((1,), (1,)), ((), ())), preferred_element_type=F32,
                )
                for h in range(2):
                    w32[pl.ds(p * 4 + tt * 2 + h, 256, stride=8), :] = o[:, h * 128 : (h + 1) * 128]

        @pl.loop(0, n)
        def _(k):
            rows = w32[pl.ds(pl.multiple_of(k * 128, 128), 128), :]
            wb[fb, k] = rows.reshape(n, 8, 128).astype(BF16)

    def zcopy(fb, d):
        to = stn_at(d)
        return pltpu.make_async_remote_copy(
            wb.at[fb, to], rz.at[fb, sk], zsend.at[fb, d], zrecv.at[fb, d],
            device_id={"stn": to}, device_id_type=MESH,
        )

    def zlocal(fb):
        return pltpu.make_async_copy(wb.at[fb, sk], rz.at[fb, sk], lsem.at[0, fb])

    def ccopy(fb, d):
        to = chan_at(d)
        return pltpu.make_async_remote_copy(
            rz.at[fb, :, to], bb.at[fb, ci], csend.at[fb, d], crecv.at[fb, d],
            device_id={"chan": to}, device_id_type=MESH,
        )

    def clocal(fb):
        return pltpu.make_async_copy(rz.at[fb, :, ci], bb.at[fb, ci], lsem.at[1, fb])

    def mcopy(d):
        to = stn_at(d)
        return pltpu.make_async_remote_copy(
            mask_ref.at[to], mk.at[sk], msend.at[d], mrecv.at[d],
            device_id={"stn": to}, device_id_type=MESH,
        )

    mlocal = pltpu.make_async_copy(mask_ref.at[sk], mk.at[sk], lsem.at[2, 0])

    def hcopy(part):
        first, count = ((8, 7), (0, 8))[part]
        return pltpu.make_async_remote_copy(
            v_ref.at[:, pl.ds((own - halo + first) * nfft, count * nfft)],
            ext.at[:, pl.ds(first * nfft, count * nfft)],
            hsend.at[part], hrecv.at[part],
            device_id={"chan": lax.rem(ci + 1, n)}, device_id_type=MESH,
        )

    def zstart(fb):
        zlocal(fb).start()

        @pl.loop(1, n)
        def _(d):
            zcopy(fb, d).start()

    def cstart(fb):
        zlocal(fb).wait()

        @pl.loop(1, n)
        def _(d):
            zcopy(fb, d).wait_recv()

        clocal(fb).start()

        @pl.loop(1, n)
        def _(d):
            ccopy(fb, d).start()

    def halo_wait(part):
        first, count = ((8, 7), (0, 8))[part]

        @pl.when(ci > 0)
        def _():
            hcopy(part).wait_recv()

        @pl.when(ci == 0)
        def _():
            ext[:, first * nfft : (first + count) * nfft] = jnp.zeros((64, count * nfft), BF16)

    load.wait()
    fir(2)
    pl.semaphore_wait(bar, 2 * (n - 1))

    @pl.when(ci < n - 1)
    def _():
        hcopy(0).start()
        hcopy(1).start()

    mlocal.start()

    @pl.loop(1, n)
    def _(d):
        mcopy(d).start()

    dft(2)
    zstart(2)
    halo_wait(0)
    fir(1)
    dft(1)
    zstart(1)
    halo_wait(1)
    fir(0)
    dft(0)
    zstart(0)

    mlocal.wait()

    @pl.loop(1, n)
    def _(d):
        mcopy(d).wait_recv()

    for fb in range(3):
        mx[fb] = jnp.dot(
            mk[...].reshape(n * n, 128), spread_ref[fb], preferred_element_type=F32
        )

    lane = lax.broadcasted_iota(jnp.int32, (128, 128), 1)
    low = lane < 64
    row = lax.broadcasted_iota(jnp.int32, (n, 8, 128), 1)

    def assemble(fb):
        clocal(fb).wait()

        @pl.loop(1, n)
        def _(d):
            ccopy(fb, d).wait_recv()

        @pl.loop(0, n // 2)
        def _(jp):
            both = []
            for h in range(2):
                j = 2 * jp + h
                data = bb[fb, :, j].astype(F32)
                flag = mx[fb, pl.ds(pl.multiple_of(j * n, n), n), :]
                both.append((data * flag.reshape(n, 1, 128)).reshape(128, 128))
            turned = [pltpu.roll(b, 64, 1) for b in both]
            parts = [jnp.where(low, both[0], turned[1]), jnp.where(low, turned[0], both[1])]
            c0 = pl.multiple_of(jp * 128, 128)
            for h in range(2):
                z = parts[h]
                r0 = h * 384 + fb * 128
                zy[r0 : r0 + 128, pl.ds(c0, 128)] = z.astype(BF16)
                y = pltpu.roll(z.reshape(n, 8, 128), 4, 1)
                y = jnp.where(row < 4, -y, y).reshape(128, 128)
                zy[r0 : r0 + 128, pl.ds(1024 + c0, 128)] = y.astype(BF16)
                zt[pl.ds(c0, 128), r0 : r0 + 128] = z.T.astype(BF16)

    cstart(2)
    cstart(1)
    assemble(2)
    cstart(0)
    assemble(1)
    assemble(0)

    def ocopy(d):
        to = stn_at(d)
        return pltpu.make_async_remote_copy(
            sb.at[to], o_ref.at[sk], osend.at[d], orecv.at[d],
            device_id={"stn": to}, device_id_type=MESH,
        )

    olocal = pltpu.make_async_copy(sb.at[sk], o_ref.at[sk], lsem.at[2, 1])
    scale = 1.0 / (own * n)

    for step in (2, 1, 3, 0):
        g = lax.rem(sk // 4 + step, 4)
        rows = zt[pl.ds(pl.multiple_of(g * 256, 256), 256), :]
        for col in range(8):
            o = jnp.dot(rows, zy[:, col * 256 : (col + 1) * 256], preferred_element_type=F32)
            o = (o * scale).astype(BF16).reshape(4, 64, 256)
            p, c = divmod(col, 4)
            sb[pl.ds(g * 4, 4), p, :, c * 256 : (c + 1) * 256] = o

        @pl.loop(0, 4)
        def _(jj):
            d = lax.rem(g * 4 + jj - sk + n, n)

            @pl.when(d > 0)
            def _():
                ocopy(d).start()

            @pl.when(d == 0)
            def _():
                olocal.start()

    @pl.when(ci < n - 1)
    def _():
        hcopy(0).wait_send()
        hcopy(1).wait_send()

    @pl.loop(1, n)
    def _(d):
        mcopy(d).wait_send()
        for fb in range(3):
            zcopy(fb, d).wait_send()
            ccopy(fb, d).wait_send()

    olocal.wait()

    @pl.loop(1, n)
    def _(d):
        ocopy(d).wait_send()
        ocopy(d).wait_recv()


def shards(voltages, pfb_taps, flags):
    n = lax.axis_size("stn")
    table = jnp.asarray(dft_table(pfb_taps.shape[1], n, n))
    hot = jnp.asarray(spread(flags.shape[0], 3, 128))
    keep = jnp.transpose(flags, (1, 2, 0)).reshape(n, n, 3 * flags.shape[0]).astype(BF16)
    keep = jnp.pad(keep, ((0, 0), (0, 0), (0, 128 - 3 * flags.shape[0])))
    vm = pl.BlockSpec(memory_space=pltpu.VMEM)
    anywhere = pl.BlockSpec(memory_space=pl.ANY)
    dma = pltpu.SemaphoreType.DMA
    rows = pl.pallas_call(
        functools.partial(kernel, n),
        out_shape=jax.ShapeDtypeStruct((n, 2, 64, 1024), BF16),
        in_specs=[anywhere, vm, vm, vm, vm],
        out_specs=anywhere,
        scratch_shapes=[
            pltpu.VMEM((64, 39 * 512), BF16),
            pltpu.VMEM((512, 512), BF16),
            pltpu.VMEM((2048, 128), F32),
            pltpu.VMEM((3, n, n, 8, 128), BF16),
            pltpu.VMEM((3, n, n, 8, 128), BF16),
            pltpu.VMEM((3, n, n, 8, 128), BF16),
            pltpu.VMEM((n, n, 128), BF16),
            pltpu.VMEM((3, n * n, 128), F32),
            pltpu.VMEM((768, 2048), BF16),
            pltpu.VMEM((1024, 768), BF16),
            pltpu.VMEM((n, 2, 64, 1024), BF16),
            dma, dma((2,)), dma((2,)), dma((n,)), dma((n,)), dma((3, n)), dma((3, n)),
            dma((3, n)), dma((3, n)), dma((n,)), dma((n,)), dma((3, 3)),
        ],
        compiler_params=pltpu.CompilerParams(
            collective_id=0, has_side_effects=True, vmem_limit_bytes=56 << 20
        ),
        name="correlate",
    )(voltages, pfb_taps, table, keep, hot)
    return rows.astype(F32)


def solution(mesh):
    placed = (P("stn", "chan"), P(), P("stn", "chan", None))
    return jax.shard_map(
        shards, mesh=mesh, in_specs=placed, out_specs=P("chan", None, "stn", None), check_vma=False
    )
```

```python
import functools
import math

import jax
import jax.numpy as jnp
import ml_dtypes
import numpy as np
from jax import lax
from jax.experimental import pallas as pl
from jax.experimental.pallas import tpu as pltpu
from jax.sharding import PartitionSpec as P

POLS = 2
BF16 = jnp.bfloat16
F32 = jnp.float32
MESH = pl.DeviceIdType.MESH


def dft_table(length):
    sample = np.arange(length)
    phase = (np.arange(length // 2)[:, None] * sample[None, :]) % length
    angles = (phase.astype(np.float32) * np.float32(2.0 * math.pi / length)).astype(np.float64)
    values = np.concatenate([np.cos(angles), -np.sin(angles)], axis=0)
    return (values.astype(np.float32) / np.float32(math.sqrt(length))).astype(ml_dtypes.bfloat16)


def spread(stations, blocks, lanes):
    out = np.zeros((blocks, lanes, lanes), np.float32)
    for fb in range(blocks):
        for lane in range(lanes):
            out[fb, fb * stations + (lane % (lanes // 2)) // POLS, lane] = 1.0
    return out.astype(ml_dtypes.bfloat16)


def kernel(
    n,
    v_ref, taps_ref, tab_ref, mask_ref, spread_ref,
    o_ref,
    ext, filt, w32, wb, rx, mk, mx, zo, lt, zr, ob, mb,
    vsem, hsend, hrecv, msend, mrecv, xsend, xrecv, zsend, zrecv, osend, orecv, bsend, brecv, lsem, olsem,
):
    ci = lax.axis_index("chan")
    sk = lax.axis_index("stn")
    nfft = 512
    halo = 15
    own = v_ref.shape[1] // nfft
    planes = n // 2
    z = sk // 2
    h = lax.rem(sk, 2)

    def at(dz, hh):
        return lax.rem(z + dz + planes, planes) * 2 + hh

    load = pltpu.make_async_copy(v_ref, ext.at[:, halo * nfft :], vsem)
    load.start()

    bar = pltpu.get_barrier_semaphore()

    def greet(chan, stn):
        pl.semaphore_signal(bar, inc=1, device_id={"chan": chan, "stn": stn}, device_id_type=MESH)

    @pl.loop(1, 2 * n)
    def _(e):
        greet(lax.rem(ci + e // 2, n), z * 2 + lax.rem(h + e, 2))

    @pl.loop(0, 2)
    def _(hh):
        for dz in (1, -1, 2, -2, 3, -3):
            greet(ci, at(dz, hh))

    def fir(fb):
        @pl.loop(0, 16)
        def _(idx):
            s0 = pl.multiple_of((idx // 4) * 16, 16)
            n0 = pl.multiple_of(lax.rem(idx, 4) * 128, 128)
            taps = [taps_ref[pl.ds(k, 1), pl.ds(n0, 128)] for k in range(16)]
            x = [
                ext[pl.ds(s0, 16), pl.ds(pl.multiple_of((fb * 8 + f) * nfft + n0, 128), 128)].astype(F32)
                for f in range(23)
            ]
            for t in range(8):
                acc = taps[0] * x[t + 15]
                for k in range(1, 16):
                    acc = acc + taps[k] * x[t + 15 - k]
                filt[pl.ds(pl.multiple_of(t * 64 + s0, 16), 16), pl.ds(n0, 128)] = acc.astype(BF16)

    def dft(fb):
        for tt in range(2):
            for p in range(2):
                o = lax.dot_general(
                    tab_ref[p * 256 : (p + 1) * 256, :], filt[tt * 256 : (tt + 1) * 256, :],
                    (((1,), (1,)), ((), ())), preferred_element_type=F32,
                )
                for half in range(2):
                    w32[pl.ds(p * 4 + tt * 2 + half, 256, stride=8), :] = o[:, half * 128 : (half + 1) * 128]

        @pl.loop(0, n)
        def _(i):
            rows = w32[pl.ds(pl.multiple_of(i * 128, 128), 128), :]
            wb[fb, i] = rows.reshape(2, n // 2, 8, 128).astype(BF16)

    def xcopy(fb, e):
        chan = lax.rem(ci + e // 2, n)
        hh = lax.rem(h + e, 2)
        return pltpu.make_async_remote_copy(
            wb.at[fb, chan, hh], rx.at[fb, h, ci], xsend.at[fb, e], xrecv.at[fb, e],
            device_id={"chan": chan, "stn": z * 2 + hh}, device_id_type=MESH,
        )

    def xlocal(fb):
        return pltpu.make_async_copy(wb.at[fb, ci, h], rx.at[fb, h, ci], lsem.at[fb])

    mcopy = pltpu.make_async_remote_copy(
        mask_ref.at[1 - h], mk.at[h], msend, mrecv,
        device_id={"chan": ci, "stn": z * 2 + 1 - h}, device_id_type=MESH,
    )
    mlocal = pltpu.make_async_copy(mask_ref.at[h], mk.at[h], lsem.at[3])

    def hcopy(part):
        first, count = ((8, 7), (0, 8))[part]
        return pltpu.make_async_remote_copy(
            v_ref.at[:, pl.ds((own - halo + first) * nfft, count * nfft)],
            ext.at[:, pl.ds(first * nfft, count * nfft)],
            hsend.at[part], hrecv.at[part],
            device_id={"chan": lax.rem(ci + 1, n), "stn": sk}, device_id_type=MESH,
        )

    def xstart(fb):
        xlocal(fb).start()

        @pl.loop(1, 2 * n)
        def _(e):
            xcopy(fb, e).start()

    def halo_wait(part):
        first, count = ((8, 7), (0, 8))[part]

        @pl.when(ci > 0)
        def _():
            hcopy(part).wait_recv()

        @pl.when(ci == 0)
        def _():
            ext[:, first * nfft : (first + count) * nfft] = jnp.zeros((64, count * nfft), BF16)

    lane = lax.broadcasted_iota(jnp.int32, (128, 128), 1)
    low = lane < 64
    row = lax.broadcasted_iota(jnp.int32, (n, 8, 128), 1)

    def zcopy(way, s, fb):
        src = zo.at[pl.ds(way * 4, 4)] if s == 0 else zr.at[way, s - 1]
        part = pl.ds(fb * 256, 256)
        return pltpu.make_async_remote_copy(
            src.at[:, part, :], zr.at[way, s, :, part, :], zsend.at[way, s, fb], zrecv.at[way, s, fb],
            device_id={"chan": ci, "stn": at(1 - 2 * way, h)}, device_id_type=MESH,
        )

    def assemble(fb):
        xlocal(fb).wait()

        @pl.loop(1, 2 * n)
        def _(e):
            xcopy(fb, e).wait_recv()

        @pl.loop(0, 8)
        def _(q):
            both = []
            for hh in range(2):
                data = rx[fb, hh, :, q].astype(F32)
                flag = mx[fb, pl.ds(pl.multiple_of((hh * 8 + q) * n, n), n), :]
                both.append((data * flag.reshape(n, 1, 128)).reshape(128, 128))
            turned = [pltpu.roll(b, 64, 1) for b in both]
            zo[q, fb * 256 : fb * 256 + 128, :] = jnp.where(low, both[0], turned[1]).astype(BF16)
            zo[q, fb * 256 + 128 : fb * 256 + 256, :] = jnp.where(low, turned[0], both[1]).astype(BF16)

        for way in range(2):
            zcopy(way, 0, fb).start()

    def turn(fb):
        @pl.loop(0, 8)
        def _(q):
            for part in range(2):
                r0 = fb * 256 + part * 128
                b = zo[q, r0 : r0 + 128, :].astype(F32)
                y = pltpu.roll(b.reshape(n, 8, 128), 4, 1)
                y = jnp.where(row < 4, y, -y).reshape(128, 128)
                lt[q, 0:128, r0 : r0 + 128] = b.T.astype(BF16)
                lt[q, 128:256, r0 : r0 + 128] = y.T.astype(BF16)

    load.wait()
    fir(2)
    dft(2)
    pl.semaphore_wait(bar, 2 * n - 1 + 12)

    @pl.when(ci < n - 1)
    def _():
        hcopy(0).start()

    mlocal.start()
    mcopy.start()
    xstart(2)

    @pl.when(ci < n - 1)
    def _():
        hcopy(1).start()

    mlocal.wait()
    mcopy.wait_recv()
    for fb in range(3):
        mx[fb] = jnp.dot(mk[...].reshape(n * n, 128), spread_ref[fb], preferred_element_type=F32)

    halo_wait(0)
    fir(1)
    dft(1)
    xstart(1)
    assemble(2)
    halo_wait(1)
    fir(0)
    dft(0)
    xstart(0)
    assemble(1)
    turn(2)
    assemble(0)
    turn(1)
    turn(0)

    scale = 1.0 / (own * n)

    def home(way):
        return pl.ds(h * 8 + way * 4, 4)

    def lanes(dz):
        return pl.ds(pl.multiple_of(lax.rem(z + dz + planes, planes) * 128, 128), 128)

    def shift(way, s):
        return s if way == 1 else -s

    def olocal(way, s):
        return pltpu.make_async_copy(
            ob.at[way, s, h], o_ref.at[home(way), :, :, lanes(shift(way, s))], olsem.at[way, s]
        )

    def ocopy(way, s):
        return pltpu.make_async_remote_copy(
            ob.at[way, s, 1 - h], o_ref.at[home(way), :, :, lanes(shift(way, s))],
            osend.at[way, s], orecv.at[way, s],
            device_id={"chan": ci, "stn": z * 2 + 1 - h}, device_id_type=MESH,
        )

    def bcopy(way, s, hh):
        return pltpu.make_async_remote_copy(
            mb.at[way, s - 1, hh], o_ref.at[home(way), :, :, lanes(0)],
            bsend.at[way, s - 1, hh], brecv.at[way, s - 1, h],
            device_id={"chan": ci, "stn": at(shift(way, s), hh)}, device_id_type=MESH,
        )

    def correlate(way, s):
        @pl.loop(0, 4)
        def _(q):
            block = zo[way * 4 + q] if s == 0 else zr[way, s - 1, q]
            o = jnp.dot(lt[way * 4 + q], block, preferred_element_type=F32) * scale
            rows = o.astype(BF16).reshape(2, 2, 64, 128)
            for p in range(2):
                for hh in range(2):
                    ob[way, s, hh, q, p] = rows[p, hh]
            if 0 < s < 4:
                back = (o[0:128].T.astype(BF16), (-o[128:256]).T.astype(BF16))
                for p in range(2):
                    for hh in range(2):
                        mb[way, s - 1, hh, q, p] = back[p][hh * 64 : (hh + 1) * 64]

        olocal(way, s).start()
        ocopy(way, s).start()
        if 0 < s < 4:
            bcopy(way, s, 0).start()
            bcopy(way, s, 1).start()

    for s in range(5):
        if s > 0:
            for fb in (2, 1, 0):
                for way in range(2):
                    zcopy(way, s - 1, fb).wait_recv()
                    if s < 4:
                        zcopy(way, s, fb).start()
        correlate(0, s)
        correlate(1, s)

    @pl.when(ci < n - 1)
    def _():
        hcopy(0).wait_send()
        hcopy(1).wait_send()

    mcopy.wait_send()

    @pl.loop(1, 2 * n)
    def _(e):
        for fb in range(3):
            xcopy(fb, e).wait_send()

    for way in range(2):
        for s in range(4):
            for fb in range(3):
                zcopy(way, s, fb).wait_send()
        for s in range(5):
            olocal(way, s).wait()
            ocopy(way, s).wait_send()
            ocopy(way, s).wait_recv()
        for s in range(1, 4):
            for hh in range(2):
                bcopy(way, s, hh).wait_send()
                pltpu.make_async_remote_copy(
                    mb.at[way, s - 1, hh], o_ref.at[home(way), :, :, lanes(0)],
                    bsend.at[way, s - 1, hh], brecv.at[way, s - 1, hh],
                    device_id={"chan": ci, "stn": at(shift(way, s), hh)}, device_id_type=MESH,
                ).wait_recv()


def shards(voltages, pfb_taps, flags):
    n = lax.axis_size("stn")
    table = jnp.asarray(dft_table(pfb_taps.shape[1]))
    hot = jnp.asarray(spread(flags.shape[0], 3, 128))
    keep = jnp.transpose(flags, (1, 2, 0)).reshape(n, n, 3 * flags.shape[0]).astype(BF16)
    keep = jnp.pad(keep, ((0, 0), (0, 0), (0, 128 - 3 * flags.shape[0]))).reshape(2, n // 2, n, 128)
    vm = pl.BlockSpec(memory_space=pltpu.VMEM)
    anywhere = pl.BlockSpec(memory_space=pl.ANY)
    dma = pltpu.SemaphoreType.DMA
    rows = pl.pallas_call(
        functools.partial(kernel, n),
        out_shape=jax.ShapeDtypeStruct((n, 2, 64, 1024), BF16),
        in_specs=[anywhere, vm, vm, vm, vm],
        out_specs=anywhere,
        scratch_shapes=[
            pltpu.VMEM((64, 39 * 512), BF16),
            pltpu.VMEM((512, 512), BF16),
            pltpu.VMEM((2048, 128), F32),
            pltpu.VMEM((3, n, 2, n // 2, 8, 128), BF16),
            pltpu.VMEM((3, 2, n, n // 2, 8, 128), BF16),
            pltpu.VMEM((2, n // 2, n, 128), BF16),
            pltpu.VMEM((3, n * n, 128), F32),
            pltpu.VMEM((8, 768, 128), BF16),
            pltpu.VMEM((8, 256, 768), BF16),
            pltpu.VMEM((2, 4, 4, 768, 128), BF16),
            pltpu.VMEM((2, 5, 2, 4, 2, 64, 128), BF16),
            pltpu.VMEM((2, 3, 2, 4, 2, 64, 128), BF16),
            dma, dma((2,)), dma((2,)), dma, dma, dma((3, 2 * n)), dma((3, 2 * n)),
            dma((2, 4, 3)), dma((2, 4, 3)), dma((2, 5)), dma((2, 5)),
            dma((2, 3, 2)), dma((2, 3, 2)), dma((4,)), dma((2, 5)),
        ],
        compiler_params=pltpu.CompilerParams(
            collective_id=0, has_side_effects=True, vmem_limit_bytes=56 << 20
        ),
        name="correlate",
    )(voltages, pfb_taps, table, keep, hot)
    return rows.astype(F32)


def solution(mesh):
    placed = (P("stn", "chan"), P(), P("stn", "chan", None))
    return jax.shard_map(
        shards, mesh=mesh, in_specs=placed, out_specs=P("chan", None, "stn", None), check_vma=False
    )
```

```python
import functools
import math

import jax
import jax.numpy as jnp
import ml_dtypes
import numpy as np
from jax import lax
from jax.experimental import pallas as pl
from jax.experimental.pallas import tpu as pltpu
from jax.sharding import PartitionSpec as P

POLS = 2
BF16 = jnp.bfloat16
F32 = jnp.float32
MESH = pl.DeviceIdType.MESH


def dft_table(length):
    sample = np.arange(length)
    phase = (np.arange(length // 2)[:, None] * sample[None, :]) % length
    angles = (phase.astype(np.float32) * np.float32(2.0 * math.pi / length)).astype(np.float64)
    values = np.concatenate([np.cos(angles), -np.sin(angles)], axis=0)
    return (values.astype(np.float32) / np.float32(math.sqrt(length))).astype(ml_dtypes.bfloat16)


def spread(stations, blocks, lanes):
    out = np.zeros((blocks, blocks * stations, lanes), np.float32)
    for fb in range(blocks):
        for lane in range(lanes):
            out[fb, fb * stations + (lane % (lanes // 2)) // POLS, lane] = 1.0
    return out.astype(ml_dtypes.bfloat16)


def kernel(
    n,
    v_ref, taps_ref, tab_ref, mask_ref, spread_ref,
    o_ref,
    ext, filt, w32, wb, rx, mk, mx, zo, lt, zr, ob, mb,
    vsem, hsend, hrecv, msend, mrecv, xsend, xrecv, zsend, zrecv, osend, orecv, bsend, brecv, lsem, olsem,
):
    ci = lax.axis_index("chan")
    sk = lax.axis_index("stn")
    nfft = 512
    halo = 15
    own = v_ref.shape[1] // nfft
    planes = n // 2
    z = sk // 2
    h = lax.rem(sk, 2)

    def at(dz, hh):
        return lax.rem(z + dz + planes, planes) * 2 + hh

    load = pltpu.make_async_copy(v_ref, ext.at[:, halo * nfft :], vsem)
    load.start()

    bar = pltpu.get_barrier_semaphore()

    def greet(chan, stn):
        pl.semaphore_signal(bar, inc=1, device_id={"chan": chan, "stn": stn}, device_id_type=MESH)

    @pl.loop(1, 2 * n)
    def _(e):
        greet(lax.rem(ci + e // 2, n), z * 2 + lax.rem(h + e, 2))

    @pl.loop(0, 2)
    def _(hh):
        for dz in (1, -1, 2, -2, 3, -3):
            greet(ci, at(dz, hh))

    def fir(fb):
        @pl.loop(0, 16)
        def _(idx):
            s0 = pl.multiple_of((idx // 4) * 16, 16)
            n0 = pl.multiple_of(lax.rem(idx, 4) * 128, 128)
            taps = [taps_ref[pl.ds(k, 1), pl.ds(n0, 128)] for k in range(16)]
            x = [
                ext[pl.ds(s0, 16), pl.ds(pl.multiple_of((fb * 8 + f) * nfft + n0, 128), 128)].astype(F32)
                for f in range(23)
            ]
            for t in range(8):
                acc = taps[0] * x[t + 15]
                for k in range(1, 16):
                    acc = acc + taps[k] * x[t + 15 - k]
                filt[pl.ds(pl.multiple_of(t * 64 + s0, 16), 16), pl.ds(n0, 128)] = acc.astype(BF16)

    def dft(fb):
        for tt in range(2):
            for p in range(2):
                o = lax.dot_general(
                    tab_ref[p * 256 : (p + 1) * 256, :], filt[tt * 256 : (tt + 1) * 256, :],
                    (((1,), (1,)), ((), ())), preferred_element_type=F32,
                )
                for half in range(2):
                    w32[pl.ds(p * 4 + tt * 2 + half, 256, stride=8), :] = o[:, half * 128 : (half + 1) * 128]

        @pl.loop(0, n)
        def _(i):
            rows = w32[pl.ds(pl.multiple_of(i * 128, 128), 128), :]
            wb[fb, i] = rows.reshape(2, n // 2, 8, 128).astype(BF16)

    def xcopy(fb, e):
        chan = lax.rem(ci + e // 2, n)
        hh = lax.rem(h + e, 2)
        return pltpu.make_async_remote_copy(
            wb.at[fb, chan, hh], rx.at[fb, h, ci], xsend.at[fb, e], xrecv.at[fb, e],
            device_id={"chan": chan, "stn": z * 2 + hh}, device_id_type=MESH,
        )

    def xlocal(fb):
        return pltpu.make_async_copy(wb.at[fb, ci, h], rx.at[fb, h, ci], lsem.at[fb])

    mcopy = pltpu.make_async_remote_copy(
        mask_ref.at[1 - h], mk.at[h], msend, mrecv,
        device_id={"chan": ci, "stn": z * 2 + 1 - h}, device_id_type=MESH,
    )
    mlocal = pltpu.make_async_copy(mask_ref.at[h], mk.at[h], lsem.at[3])

    def hcopy(part):
        first, count = ((8, 7), (0, 8))[part]
        return pltpu.make_async_remote_copy(
            v_ref.at[:, pl.ds((own - halo + first) * nfft, count * nfft)],
            ext.at[:, pl.ds(first * nfft, count * nfft)],
            hsend.at[part], hrecv.at[part],
            device_id={"chan": lax.rem(ci + 1, n), "stn": sk}, device_id_type=MESH,
        )

    def xstart(fb):
        xlocal(fb).start()

        @pl.loop(1, 2 * n)
        def _(e):
            xcopy(fb, e).start()

    def halo_wait(part):
        first, count = ((8, 7), (0, 8))[part]

        @pl.when(ci > 0)
        def _():
            hcopy(part).wait_recv()

        @pl.when(ci == 0)
        def _():
            ext[:, first * nfft : (first + count) * nfft] = jnp.zeros((64, count * nfft), BF16)

    lane = lax.broadcasted_iota(jnp.int32, (128, 128), 1)
    low = lane < 64
    row = lax.broadcasted_iota(jnp.int32, (n, 8, 128), 1)

    def zcopy(way, s, fb):
        src = zo.at[pl.ds(way * 4, 4)] if s == 0 else zr.at[way, s - 1]
        part = pl.ds(fb * 256, 256)
        return pltpu.make_async_remote_copy(
            src.at[:, part, :], zr.at[way, s, :, part, :], zsend.at[way, s, fb], zrecv.at[way, s, fb],
            device_id={"chan": ci, "stn": at(1 - 2 * way, h)}, device_id_type=MESH,
        )

    def assemble(fb):
        xlocal(fb).wait()

        @pl.loop(1, 2 * n)
        def _(e):
            xcopy(fb, e).wait_recv()

        @pl.loop(0, 8)
        def _(q):
            both = []
            for hh in range(2):
                data = rx[fb, hh, :, q].astype(F32)
                flag = mx[fb, pl.ds(pl.multiple_of((hh * 8 + q) * n, n), n), :]
                both.append((data * flag.reshape(n, 1, 128)).reshape(128, 128))
            turned = [pltpu.roll(b, 64, 1) for b in both]
            zo[q, fb * 256 : fb * 256 + 128, :] = jnp.where(low, both[0], turned[1]).astype(BF16)
            zo[q, fb * 256 + 128 : fb * 256 + 256, :] = jnp.where(low, turned[0], both[1]).astype(BF16)

        for way in range(2):
            zcopy(way, 0, fb).start()

    def turn(fb):
        @pl.loop(0, 8)
        def _(q):
            for part in range(2):
                r0 = fb * 256 + part * 128
                b = zo[q, r0 : r0 + 128, :].astype(F32)
                y = pltpu.roll(b.reshape(n, 8, 128), 4, 1)
                y = jnp.where(row < 4, y, -y).reshape(128, 128)
                lt[q, 0:128, r0 : r0 + 128] = b.T.astype(BF16)
                lt[q, 128:256, r0 : r0 + 128] = y.T.astype(BF16)

    load.wait()
    fir(2)
    dft(2)
    pl.semaphore_wait(bar, 2 * n - 1 + 12)

    mlocal.start()
    mcopy.start()
    xstart(2)

    @pl.when(ci < n - 1)
    def _():
        hcopy(0).start()
        hcopy(1).start()

    mlocal.wait()
    mcopy.wait_recv()
    for fb in range(3):
        mx[fb] = jnp.dot(mk[...].reshape(n * n, mk.shape[3]), spread_ref[fb], preferred_element_type=F32)

    def pass_on(s, fb):
        for way in range(2):
            zcopy(way, s, fb).wait_recv()
            if s < 3:
                zcopy(way, s + 1, fb).start()

    assemble(2)
    halo_wait(0)
    fir(1)
    dft(1)
    xstart(1)
    pass_on(0, 2)
    halo_wait(1)
    fir(0)
    dft(0)
    xstart(0)
    turn(2)
    pass_on(1, 2)
    assemble(1)
    turn(1)
    pass_on(0, 1)
    pass_on(2, 2)
    assemble(0)
    turn(0)

    scale = 1.0 / (own * n)

    def home(way):
        return pl.ds(h * 8 + way * 4, 4)

    def lanes(dz):
        return pl.ds(pl.multiple_of(lax.rem(z + dz + planes, planes) * 128, 128), 128)

    def shift(way, s):
        return s if way == 1 else -s

    def olocal(way, s):
        return pltpu.make_async_copy(
            ob.at[way, s, h], o_ref.at[home(way), :, :, lanes(shift(way, s))], olsem.at[way, s]
        )

    def ocopy(way, s):
        return pltpu.make_async_remote_copy(
            ob.at[way, s, 1 - h], o_ref.at[home(way), :, :, lanes(shift(way, s))],
            osend.at[way, s], orecv.at[way, s],
            device_id={"chan": ci, "stn": z * 2 + 1 - h}, device_id_type=MESH,
        )

    def bcopy(way, s, hh):
        return pltpu.make_async_remote_copy(
            mb.at[way, s - 1, hh], o_ref.at[home(way), :, :, lanes(0)],
            bsend.at[way, s - 1, hh], brecv.at[way, s - 1, h],
            device_id={"chan": ci, "stn": at(shift(way, s), hh)}, device_id_type=MESH,
        )

    def correlate(way, s):
        @pl.loop(0, 4)
        def _(q):
            block = zo[way * 4 + q] if s == 0 else zr[way, s - 1, q]
            o = jnp.dot(lt[way * 4 + q], block, preferred_element_type=F32) * scale
            rows = o.astype(BF16).reshape(2, 2, 64, 128)
            for p in range(2):
                for hh in range(2):
                    ob[way, s, hh, q, p] = rows[p, hh]
            if 0 < s < 4:
                back = (o[0:128].T.astype(BF16), (-o[128:256]).T.astype(BF16))
                for p in range(2):
                    for hh in range(2):
                        mb[way, s - 1, hh, q, p] = back[p][hh * 64 : (hh + 1) * 64]

        olocal(way, s).start()
        ocopy(way, s).start()
        if 0 < s < 4:
            bcopy(way, s, 0).start()
            bcopy(way, s, 1).start()

    def step(s):
        correlate(0, s)
        correlate(1, s)

    pass_on(1, 1)
    step(0)
    pass_on(0, 0)
    step(1)
    pass_on(3, 2)
    pass_on(2, 1)
    pass_on(1, 0)
    step(2)
    pass_on(3, 1)
    pass_on(2, 0)
    step(3)
    pass_on(3, 0)
    step(4)

    @pl.when(ci < n - 1)
    def _():
        hcopy(0).wait_send()
        hcopy(1).wait_send()

    mcopy.wait_send()

    @pl.loop(1, 2 * n)
    def _(e):
        for fb in range(3):
            xcopy(fb, e).wait_send()

    for way in range(2):
        for s in range(4):
            for fb in range(3):
                zcopy(way, s, fb).wait_send()
        for s in range(5):
            olocal(way, s).wait()
            ocopy(way, s).wait_send()
            ocopy(way, s).wait_recv()
        for s in range(1, 4):
            for hh in range(2):
                bcopy(way, s, hh).wait_send()
                pltpu.make_async_remote_copy(
                    mb.at[way, s - 1, hh], o_ref.at[home(way), :, :, lanes(0)],
                    bsend.at[way, s - 1, hh], brecv.at[way, s - 1, hh],
                    device_id={"chan": ci, "stn": at(shift(way, s), hh)}, device_id_type=MESH,
                ).wait_recv()


def shards(voltages, pfb_taps, flags):
    n = lax.axis_size("stn")
    table = jnp.asarray(dft_table(pfb_taps.shape[1]))
    hot = jnp.asarray(spread(flags.shape[0], 3, 128))
    keep = jnp.transpose(flags, (1, 2, 0)).reshape(n, n, 3 * flags.shape[0]).astype(BF16)
    keep = keep.reshape(2, n // 2, n, 3 * flags.shape[0])
    vm = pl.BlockSpec(memory_space=pltpu.VMEM)
    anywhere = pl.BlockSpec(memory_space=pl.ANY)
    dma = pltpu.SemaphoreType.DMA
    rows = pl.pallas_call(
        functools.partial(kernel, n),
        out_shape=pltpu.VMEM((n, 2, 64, 1024), BF16),
        in_specs=[anywhere, vm, vm, vm, vm],
        out_specs=vm,
        scratch_shapes=[
            pltpu.VMEM((64, 39 * 512), BF16),
            pltpu.VMEM((512, 512), BF16),
            pltpu.VMEM((2048, 128), F32),
            pltpu.VMEM((3, n, 2, n // 2, 8, 128), BF16),
            pltpu.VMEM((3, 2, n, n // 2, 8, 128), BF16),
            pltpu.VMEM((2, n // 2, n, 3 * flags.shape[0]), BF16),
            pltpu.VMEM((3, n * n, 128), F32),
            pltpu.VMEM((8, 768, 128), BF16),
            pltpu.VMEM((8, 256, 768), BF16),
            pltpu.VMEM((2, 4, 4, 768, 128), BF16),
            pltpu.VMEM((2, 5, 2, 4, 2, 64, 128), BF16),
            pltpu.VMEM((2, 3, 2, 4, 2, 64, 128), BF16),
            dma, dma((2,)), dma((2,)), dma, dma, dma((3, 2 * n)), dma((3, 2 * n)),
            dma((2, 4, 3)), dma((2, 4, 3)), dma((2, 5)), dma((2, 5)),
            dma((2, 3, 2)), dma((2, 3, 2)), dma((4,)), dma((2, 5)),
        ],
        compiler_params=pltpu.CompilerParams(
            collective_id=0, has_side_effects=True, vmem_limit_bytes=56 << 20
        ),
        name="correlate",
    )(voltages, pfb_taps, table, keep, hot)
    return rows.astype(F32)


def solution(mesh):
    placed = (P("stn", "chan"), P(), P("stn", "chan", None))
    return jax.shard_map(
        shards, mesh=mesh, in_specs=placed, out_specs=P("chan", None, "stn", None), check_vma=False
    )
```

```python
import functools
import math

import jax
import jax.numpy as jnp
import ml_dtypes
import numpy as np
from jax import lax
from jax.experimental import pallas as pl
from jax.experimental.pallas import tpu as pltpu
from jax.sharding import PartitionSpec as P

POLS = 2
BF16 = jnp.bfloat16
F32 = jnp.float32
MESH = pl.DeviceIdType.MESH


def dft_table(length):
    sample = np.arange(length)
    phase = (np.arange(length // 2)[:, None] * sample[None, :]) % length
    angles = (phase.astype(np.float32) * np.float32(2.0 * math.pi / length)).astype(np.float64)
    values = np.concatenate([np.cos(angles), -np.sin(angles)], axis=0)
    return (values.astype(np.float32) / np.float32(math.sqrt(length))).astype(ml_dtypes.bfloat16)


def spread(stations, blocks, lanes):
    out = np.zeros((blocks, blocks * stations, lanes), np.float32)
    for fb in range(blocks):
        for lane in range(lanes):
            out[fb, fb * stations + (lane % (lanes // 2)) // POLS, lane] = 1.0
    return out.astype(ml_dtypes.bfloat16)


def kernel(
    n,
    v_ref, taps_ref, tab_ref, flags_ref, spread_ref,
    o_ref,
    fcol, mask_ref, ext, filt, w32, wb, rx, mk, mx, zo, lt, zr, ob, mb,
    vsem, hsend, hrecv, msend, mrecv, xsend, xrecv, zsend, zrecv, osend, orecv, bsend, brecv, lsem, olsem,
):
    ci = lax.axis_index("chan")
    sk = lax.axis_index("stn")
    nfft = 512
    halo = 15
    own = v_ref.shape[1] // nfft
    planes = n // 2
    z = sk // 2
    h = lax.rem(sk, 2)

    def at(dz, hh):
        return lax.rem(z + dz + planes, planes) * 2 + hh

    load = pltpu.make_async_copy(v_ref, ext.at[:, halo * nfft :], vsem)
    load.start()

    bar = pltpu.get_barrier_semaphore()

    def greet(chan, stn):
        pl.semaphore_signal(bar, inc=1, device_id={"chan": chan, "stn": stn}, device_id_type=MESH)

    @pl.loop(1, 2 * n)
    def _(e):
        greet(lax.rem(ci + e // 2, n), z * 2 + lax.rem(h + e, 2))

    @pl.loop(0, 2)
    def _(hh):
        for dz in (1, -1, 2, -2, 3, -3):
            greet(ci, at(dz, hh))

    def fir(fb):
        @pl.loop(0, 16)
        def _(idx):
            s0 = pl.multiple_of((idx // 4) * 16, 16)
            n0 = pl.multiple_of(lax.rem(idx, 4) * 128, 128)
            taps = [taps_ref[pl.ds(k, 1), pl.ds(n0, 128)] for k in range(16)]
            x = [
                ext[pl.ds(s0, 16), pl.ds(pl.multiple_of((fb * 8 + f) * nfft + n0, 128), 128)].astype(F32)
                for f in range(23)
            ]
            for t in range(8):
                acc = taps[0] * x[t + 15]
                for k in range(1, 16):
                    acc = acc + taps[k] * x[t + 15 - k]
                filt[pl.ds(pl.multiple_of(t * 64 + s0, 16), 16), pl.ds(n0, 128)] = acc.astype(BF16)

    def dft(fb):
        for tt in range(2):
            for p in range(2):
                o = lax.dot_general(
                    tab_ref[p * 256 : (p + 1) * 256, :], filt[tt * 256 : (tt + 1) * 256, :],
                    (((1,), (1,)), ((), ())), preferred_element_type=F32,
                )
                for half in range(2):
                    w32[pl.ds(p * 4 + tt * 2 + half, 256, stride=8), :] = o[:, half * 128 : (half + 1) * 128]

        @pl.loop(0, n)
        def _(i):
            rows = w32[pl.ds(pl.multiple_of(i * 128, 128), 128), :]
            wb[fb, i] = rows.reshape(2, n // 2, 8, 128).astype(BF16)

    def xcopy(fb, e):
        chan = lax.rem(ci + e // 2, n)
        hh = lax.rem(h + e, 2)
        return pltpu.make_async_remote_copy(
            wb.at[fb, chan, hh], rx.at[fb, h, ci], xsend.at[fb, e], xrecv.at[fb, e],
            device_id={"chan": chan, "stn": z * 2 + hh}, device_id_type=MESH,
        )

    def xlocal(fb):
        return pltpu.make_async_copy(wb.at[fb, ci, h], rx.at[fb, h, ci], lsem.at[fb])

    mcopy = pltpu.make_async_remote_copy(
        mask_ref.at[1 - h], mk.at[h], msend, mrecv,
        device_id={"chan": ci, "stn": z * 2 + 1 - h}, device_id_type=MESH,
    )
    mlocal = pltpu.make_async_copy(mask_ref.at[h], mk.at[h], lsem.at[3])

    def hcopy(part):
        first, count = ((8, 7), (0, 8))[part]
        return pltpu.make_async_remote_copy(
            v_ref.at[:, pl.ds((own - halo + first) * nfft, count * nfft)],
            ext.at[:, pl.ds(first * nfft, count * nfft)],
            hsend.at[part], hrecv.at[part],
            device_id={"chan": lax.rem(ci + 1, n), "stn": sk}, device_id_type=MESH,
        )

    def xstart(fb):
        xlocal(fb).start()

        @pl.loop(1, 2 * n)
        def _(e):
            xcopy(fb, e).start()

    def halo_wait(part):
        first, count = ((8, 7), (0, 8))[part]

        @pl.when(ci > 0)
        def _():
            hcopy(part).wait_recv()

        @pl.when(ci == 0)
        def _():
            ext[:, first * nfft : (first + count) * nfft] = jnp.zeros((64, count * nfft), BF16)

    lane = lax.broadcasted_iota(jnp.int32, (128, 128), 1)
    low = lane < 64
    row = lax.broadcasted_iota(jnp.int32, (n, 8, 128), 1)

    def zcopy(way, s, fb):
        src = zo.at[pl.ds(way * 4, 4)] if s == 0 else zr.at[way, s - 1]
        part = pl.ds(fb * 256, 256)
        return pltpu.make_async_remote_copy(
            src.at[:, part, :], zr.at[way, s, :, part, :], zsend.at[way, s, fb], zrecv.at[way, s, fb],
            device_id={"chan": ci, "stn": at(1 - 2 * way, h)}, device_id_type=MESH,
        )

    def assemble(fb):
        xlocal(fb).wait()

        @pl.loop(1, 2 * n)
        def _(e):
            xcopy(fb, e).wait_recv()

        @pl.loop(0, 8)
        def _(q):
            both = []
            for hh in range(2):
                data = rx[fb, hh, :, q].astype(F32)
                flag = mx[fb, pl.ds(pl.multiple_of((hh * 8 + q) * n, n), n), :]
                both.append((data * flag.reshape(n, 1, 128)).reshape(128, 128))
            turned = [pltpu.roll(b, 64, 1) for b in both]
            zo[q, fb * 256 : fb * 256 + 128, :] = jnp.where(low, both[0], turned[1]).astype(BF16)
            zo[q, fb * 256 + 128 : fb * 256 + 256, :] = jnp.where(low, turned[0], both[1]).astype(BF16)

        for way in range(2):
            zcopy(way, 0, fb).start()

    def turn(fb):
        @pl.loop(0, 8)
        def _(q):
            for part in range(2):
                r0 = fb * 256 + part * 128
                b = zo[q, r0 : r0 + 128, :].astype(F32)
                y = pltpu.roll(b.reshape(n, 8, 128), 4, 1)
                y = jnp.where(row < 4, y, -y).reshape(128, 128)
                lt[q, 0:128, r0 : r0 + 128] = b.T.astype(BF16)
                lt[q, 128:256, r0 : r0 + 128] = y.T.astype(BF16)

    stations = flags_ref.shape[0]
    for c in range(n):
        fcol[...] = flags_ref[:, c, :].astype(F32).T
        for fb in range(3):
            mask_ref[c // (n // 2), c % (n // 2), :, fb * stations : (fb + 1) * stations] = fcol[
                pl.ds(fb, n, stride=3), :
            ].astype(BF16)

    load.wait()
    fir(2)
    dft(2)
    pl.semaphore_wait(bar, 2 * n - 1 + 12)

    mlocal.start()
    mcopy.start()
    xstart(2)

    @pl.when(ci < n - 1)
    def _():
        hcopy(0).start()
        hcopy(1).start()

    mlocal.wait()
    mcopy.wait_recv()
    for fb in range(3):
        mx[fb] = jnp.dot(mk[...].reshape(n * n, mk.shape[3]), spread_ref[fb], preferred_element_type=F32)

    def pass_on(s, fb):
        for way in range(2):
            zcopy(way, s, fb).wait_recv()
            if s < 3:
                zcopy(way, s + 1, fb).start()

    assemble(2)
    halo_wait(0)
    fir(1)
    dft(1)
    xstart(1)
    pass_on(0, 2)
    halo_wait(1)
    fir(0)
    dft(0)
    xstart(0)
    turn(2)
    pass_on(1, 2)
    assemble(1)
    turn(1)
    pass_on(0, 1)
    pass_on(2, 2)
    assemble(0)
    turn(0)

    scale = 1.0 / (own * n)

    def home(way):
        return pl.ds(h * 8 + way * 4, 4)

    def lanes(dz):
        return pl.ds(pl.multiple_of(lax.rem(z + dz + planes, planes) * 128, 128), 128)

    def shift(way, s):
        return s if way == 1 else -s

    def olocal(way, s):
        return pltpu.make_async_copy(
            ob.at[way, s, h], o_ref.at[home(way), :, :, lanes(shift(way, s))], olsem.at[way, s]
        )

    def ocopy(way, s):
        return pltpu.make_async_remote_copy(
            ob.at[way, s, 1 - h], o_ref.at[home(way), :, :, lanes(shift(way, s))],
            osend.at[way, s], orecv.at[way, s],
            device_id={"chan": ci, "stn": z * 2 + 1 - h}, device_id_type=MESH,
        )

    def bcopy(way, s, hh):
        return pltpu.make_async_remote_copy(
            mb.at[way, s - 1, hh], o_ref.at[home(way), :, :, lanes(0)],
            bsend.at[way, s - 1, hh], brecv.at[way, s - 1, h],
            device_id={"chan": ci, "stn": at(shift(way, s), hh)}, device_id_type=MESH,
        )

    def correlate(way, s):
        @pl.loop(0, 4)
        def _(q):
            block = zo[way * 4 + q] if s == 0 else zr[way, s - 1, q]
            o = jnp.dot(lt[way * 4 + q], block, preferred_element_type=F32) * scale
            rows = o.astype(BF16).reshape(2, 2, 64, 128)
            for p in range(2):
                for hh in range(2):
                    ob[way, s, hh, q, p] = rows[p, hh]
            if 0 < s < 4:
                back = (o[0:128].T.astype(BF16), (-o[128:256]).T.astype(BF16))
                for p in range(2):
                    for hh in range(2):
                        mb[way, s - 1, hh, q, p] = back[p][hh * 64 : (hh + 1) * 64]

        olocal(way, s).start()
        ocopy(way, s).start()
        if 0 < s < 4:
            bcopy(way, s, 0).start()
            bcopy(way, s, 1).start()

    def step(s):
        correlate(0, s)
        correlate(1, s)

    pass_on(1, 1)
    step(0)
    pass_on(0, 0)
    step(1)
    pass_on(3, 2)
    pass_on(2, 1)
    pass_on(1, 0)
    step(2)
    pass_on(3, 1)
    pass_on(2, 0)
    step(3)
    @pl.when(ci < n - 1)
    def _():
        hcopy(0).wait_send()
        hcopy(1).wait_send()

    mcopy.wait_send()

    @pl.loop(1, 2 * n)
    def _(e):
        for fb in range(3):
            xcopy(fb, e).wait_send()

    pass_on(3, 0)
    step(4)


    for way in range(2):
        for s in range(4):
            for fb in range(3):
                zcopy(way, s, fb).wait_send()
        for s in range(5):
            olocal(way, s).wait()
            ocopy(way, s).wait_send()
            ocopy(way, s).wait_recv()
        for s in range(1, 4):
            for hh in range(2):
                bcopy(way, s, hh).wait_send()
                pltpu.make_async_remote_copy(
                    mb.at[way, s - 1, hh], o_ref.at[home(way), :, :, lanes(0)],
                    bsend.at[way, s - 1, hh], brecv.at[way, s - 1, hh],
                    device_id={"chan": ci, "stn": at(shift(way, s), hh)}, device_id_type=MESH,
                ).wait_recv()


def shards(voltages, pfb_taps, flags):
    n = lax.axis_size("stn")
    table = jnp.asarray(dft_table(pfb_taps.shape[1]))
    hot = jnp.asarray(spread(flags.shape[0], 3, 128))
    vm = pl.BlockSpec(memory_space=pltpu.VMEM)
    anywhere = pl.BlockSpec(memory_space=pl.ANY)
    dma = pltpu.SemaphoreType.DMA
    rows = pl.pallas_call(
        functools.partial(kernel, n),
        out_shape=pltpu.VMEM((n, 2, 64, 1024), BF16),
        in_specs=[anywhere, vm, vm, vm, vm],
        out_specs=vm,
        scratch_shapes=[
            pltpu.VMEM((48, flags.shape[0]), F32),
            pltpu.VMEM((2, n // 2, n, 3 * flags.shape[0]), BF16),
            pltpu.VMEM((64, 39 * 512), BF16),
            pltpu.VMEM((512, 512), BF16),
            pltpu.VMEM((2048, 128), F32),
            pltpu.VMEM((3, n, 2, n // 2, 8, 128), BF16),
            pltpu.VMEM((3, 2, n, n // 2, 8, 128), BF16),
            pltpu.VMEM((2, n // 2, n, 3 * flags.shape[0]), BF16),
            pltpu.VMEM((3, n * n, 128), F32),
            pltpu.VMEM((8, 768, 128), BF16),
            pltpu.VMEM((8, 256, 768), BF16),
            pltpu.VMEM((2, 4, 4, 768, 128), BF16),
            pltpu.VMEM((2, 5, 2, 4, 2, 64, 128), BF16),
            pltpu.VMEM((2, 3, 2, 4, 2, 64, 128), BF16),
            dma, dma((2,)), dma((2,)), dma, dma, dma((3, 2 * n)), dma((3, 2 * n)),
            dma((2, 4, 3)), dma((2, 4, 3)), dma((2, 5)), dma((2, 5)),
            dma((2, 3, 2)), dma((2, 3, 2)), dma((4,)), dma((2, 5)),
        ],
        compiler_params=pltpu.CompilerParams(
            collective_id=0, has_side_effects=True, vmem_limit_bytes=56 << 20
        ),
        name="correlate",
    )(voltages, pfb_taps, table, flags, hot)
    return rows.astype(F32)


def solution(mesh):
    placed = (P("stn", "chan"), P(), P("stn", "chan", None))
    return jax.shard_map(
        shards, mesh=mesh, in_specs=placed, out_specs=P("chan", None, "stn", None), check_vma=False
    )
```

```python
import functools
import math

import jax
import jax.numpy as jnp
import ml_dtypes
import numpy as np
from jax import lax
from jax.experimental import pallas as pl
from jax.experimental.pallas import tpu as pltpu
from jax.sharding import PartitionSpec as P

POLS = 2
BF16 = jnp.bfloat16
F32 = jnp.float32
MESH = pl.DeviceIdType.MESH


def dft_table(length):
    sample = np.arange(length)
    phase = (np.arange(length // 2)[:, None] * sample[None, :]) % length
    angles = (phase.astype(np.float32) * np.float32(2.0 * math.pi / length)).astype(np.float64)
    values = np.concatenate([np.cos(angles), -np.sin(angles)], axis=0)
    return (values.astype(np.float32) / np.float32(math.sqrt(length))).astype(ml_dtypes.bfloat16)


def spread(stations, blocks, lanes):
    out = np.zeros((blocks, blocks * stations, lanes), np.float32)
    for fb in range(blocks):
        for lane in range(lanes):
            out[fb, fb * stations + (lane % (lanes // 2)) // POLS, lane] = 1.0
    return out.astype(ml_dtypes.bfloat16)


def kernel(
    n,
    v_ref, taps_in, tab_in, flags_in, spread_in,
    o_ref,
    taps_ref, tab_ref, flags_ref, spread_ref, fcol, mask_ref, ext, filt, w32, wb, rx, mk, mx, zo, lt, zr, ob, mb,
    vsem, hsend, hrecv, msend, mrecv, xsend, xrecv, zsend, zrecv, osend, orecv, bsend, brecv, lsem, olsem, isem,
):
    ci = lax.axis_index("chan")
    sk = lax.axis_index("stn")
    nfft = 512
    halo = 15
    own = v_ref.shape[1] // nfft
    planes = n // 2
    z = sk // 2
    h = lax.rem(sk, 2)

    def at(dz, hh):
        return lax.rem(z + dz + planes, planes) * 2 + hh

    bar = pltpu.get_barrier_semaphore()

    def greet(chan, stn):
        pl.semaphore_signal(bar, inc=1, device_id={"chan": chan, "stn": stn}, device_id_type=MESH)

    @pl.loop(0, 2)
    def _(hh):
        for dz in (3, -3, 2, -2, 1, -1):
            greet(ci, at(dz, hh))

    @pl.loop(1, 2 * n)
    def _(e):
        greet(lax.rem(ci + e // 2, n), z * 2 + lax.rem(h + e, 2))

    load = pltpu.make_async_copy(v_ref, ext.at[:, halo * nfft :], vsem)
    load.start()
    flags_load = pltpu.make_async_copy(flags_in, flags_ref, isem.at[0])
    taps_load = pltpu.make_async_copy(taps_in, taps_ref, isem.at[1])
    tab_load = pltpu.make_async_copy(tab_in, tab_ref, isem.at[2])
    spread_load = pltpu.make_async_copy(spread_in, spread_ref, isem.at[3])
    for each in (flags_load, taps_load, tab_load, spread_load):
        each.start()

    def fir(fb):
        @pl.loop(0, 16)
        def _(idx):
            s0 = pl.multiple_of((idx // 4) * 16, 16)
            n0 = pl.multiple_of(lax.rem(idx, 4) * 128, 128)
            taps = [taps_ref[pl.ds(k, 1), pl.ds(n0, 128)] for k in range(16)]
            x = [
                ext[pl.ds(s0, 16), pl.ds(pl.multiple_of((fb * 8 + f) * nfft + n0, 128), 128)].astype(F32)
                for f in range(23)
            ]
            for t in range(8):
                acc = taps[0] * x[t + 15]
                for k in range(1, 16):
                    acc = acc + taps[k] * x[t + 15 - k]
                filt[pl.ds(pl.multiple_of(t * 64 + s0, 16), 16), pl.ds(n0, 128)] = acc.astype(BF16)

    def dft(fb):
        for tt in range(2):
            for p in range(2):
                o = lax.dot_general(
                    tab_ref[p * 256 : (p + 1) * 256, :], filt[tt * 256 : (tt + 1) * 256, :],
                    (((1,), (1,)), ((), ())), preferred_element_type=F32,
                )
                for half in range(2):
                    w32[pl.ds(p * 4 + tt * 2 + half, 256, stride=8), :] = o[:, half * 128 : (half + 1) * 128]

        @pl.loop(0, n)
        def _(i):
            rows = w32[pl.ds(pl.multiple_of(i * 128, 128), 128), :]
            wb[fb, i] = rows.reshape(2, n // 2, 8, 128).astype(BF16)

    def xcopy(fb, e):
        chan = lax.rem(ci + e // 2, n)
        hh = lax.rem(h + e, 2)
        return pltpu.make_async_remote_copy(
            wb.at[fb, chan, hh], rx.at[fb, h, ci], xsend.at[fb, e], xrecv.at[fb, e],
            device_id={"chan": chan, "stn": z * 2 + hh}, device_id_type=MESH,
        )

    def xlocal(fb):
        return pltpu.make_async_copy(wb.at[fb, ci, h], rx.at[fb, h, ci], lsem.at[fb])

    mcopy = pltpu.make_async_remote_copy(
        mask_ref.at[1 - h], mk.at[h], msend, mrecv,
        device_id={"chan": ci, "stn": z * 2 + 1 - h}, device_id_type=MESH,
    )
    mlocal = pltpu.make_async_copy(mask_ref.at[h], mk.at[h], lsem.at[3])

    def hcopy(part):
        first, count = ((8, 7), (0, 8))[part]
        return pltpu.make_async_remote_copy(
            v_ref.at[:, pl.ds((own - halo + first) * nfft, count * nfft)],
            ext.at[:, pl.ds(first * nfft, count * nfft)],
            hsend.at[part], hrecv.at[part],
            device_id={"chan": lax.rem(ci + 1, n), "stn": sk}, device_id_type=MESH,
        )

    def xstart(fb):
        xlocal(fb).start()

        @pl.loop(1, 2 * n)
        def _(e):
            xcopy(fb, e).start()

    def halo_wait(part):
        first, count = ((8, 7), (0, 8))[part]

        @pl.when(ci > 0)
        def _():
            hcopy(part).wait_recv()

        @pl.when(ci == 0)
        def _():
            ext[:, first * nfft : (first + count) * nfft] = jnp.zeros((64, count * nfft), BF16)

    lane = lax.broadcasted_iota(jnp.int32, (128, 128), 1)
    low = lane < 64
    row = lax.broadcasted_iota(jnp.int32, (n, 8, 128), 1)

    def zcopy(way, s, fb):
        src = zo.at[pl.ds(way * 4, 4)] if s == 0 else zr.at[way, s - 1]
        part = pl.ds(fb * 256, 256)
        return pltpu.make_async_remote_copy(
            src.at[:, part, :], zr.at[way, s, :, part, :], zsend.at[way, s, fb], zrecv.at[way, s, fb],
            device_id={"chan": ci, "stn": at(1 - 2 * way, h)}, device_id_type=MESH,
        )

    def assemble(fb):
        xlocal(fb).wait()

        @pl.loop(1, 2 * n)
        def _(e):
            xcopy(fb, e).wait_recv()

        @pl.loop(0, 8)
        def _(q):
            both = []
            for hh in range(2):
                data = rx[fb, hh, :, q].astype(F32)
                flag = mx[fb, pl.ds(pl.multiple_of((hh * 8 + q) * n, n), n), :]
                both.append((data * flag.reshape(n, 1, 128)).reshape(128, 128))
            turned = [pltpu.roll(b, 64, 1) for b in both]
            zo[q, fb * 256 : fb * 256 + 128, :] = jnp.where(low, both[0], turned[1]).astype(BF16)
            zo[q, fb * 256 + 128 : fb * 256 + 256, :] = jnp.where(low, turned[0], both[1]).astype(BF16)

        for way in range(2):
            zcopy(way, 0, fb).start()

    def turn(fb):
        @pl.loop(0, 8)
        def _(q):
            for part in range(2):
                r0 = fb * 256 + part * 128
                b = zo[q, r0 : r0 + 128, :].astype(F32)
                y = pltpu.roll(b.reshape(n, 8, 128), 4, 1)
                y = jnp.where(row < 4, y, -y).reshape(128, 128)
                lt[q, 0:128, r0 : r0 + 128] = b.T.astype(BF16)
                lt[q, 128:256, r0 : r0 + 128] = y.T.astype(BF16)

    flags_load.wait()
    stations = flags_ref.shape[0]
    for c in range(n):
        fcol[...] = flags_ref[:, c, :].astype(F32).T
        for fb in range(3):
            mask_ref[c // (n // 2), c % (n // 2), :, fb * stations : (fb + 1) * stations] = fcol[
                pl.ds(fb, n, stride=3), :
            ].astype(BF16)

    load.wait()
    taps_load.wait()
    fir(2)
    tab_load.wait()
    spread_load.wait()
    dft(2)
    pl.semaphore_wait(bar, 2 * n - 1 + 12)

    mlocal.start()
    mcopy.start()
    xstart(2)

    @pl.when(ci < n - 1)
    def _():
        hcopy(0).start()
        hcopy(1).start()

    mlocal.wait()
    mcopy.wait_recv()
    for fb in range(3):
        mx[fb] = jnp.dot(mk[...].reshape(n * n, mk.shape[3]), spread_ref[fb], preferred_element_type=F32)

    def pass_on(s, fb):
        for way in range(2):
            zcopy(way, s, fb).wait_recv()
            if s < 3:
                zcopy(way, s + 1, fb).start()

    assemble(2)
    halo_wait(0)
    fir(1)
    dft(1)
    xstart(1)
    pass_on(0, 2)
    halo_wait(1)
    fir(0)
    dft(0)
    xstart(0)
    turn(2)
    pass_on(1, 2)
    assemble(1)
    turn(1)
    pass_on(0, 1)
    pass_on(2, 2)
    assemble(0)
    turn(0)

    scale = 1.0 / (own * n)

    def home(way):
        return pl.ds(h * 8 + way * 4, 4)

    def lanes(dz):
        return pl.ds(pl.multiple_of(lax.rem(z + dz + planes, planes) * 128, 128), 128)

    def shift(way, s):
        return s if way == 1 else -s

    def olocal(way, s):
        return pltpu.make_async_copy(
            ob.at[way, s, h], o_ref.at[home(way), :, :, lanes(shift(way, s))], olsem.at[way, s]
        )

    def ocopy(way, s):
        return pltpu.make_async_remote_copy(
            ob.at[way, s, 1 - h], o_ref.at[home(way), :, :, lanes(shift(way, s))],
            osend.at[way, s], orecv.at[way, s],
            device_id={"chan": ci, "stn": z * 2 + 1 - h}, device_id_type=MESH,
        )

    def bcopy(way, s, hh):
        return pltpu.make_async_remote_copy(
            mb.at[way, s - 1, hh], o_ref.at[home(way), :, :, lanes(0)],
            bsend.at[way, s - 1, hh], brecv.at[way, s - 1, h],
            device_id={"chan": ci, "stn": at(shift(way, s), hh)}, device_id_type=MESH,
        )

    def correlate(way, s):
        @pl.loop(0, 4)
        def _(q):
            block = zo[way * 4 + q] if s == 0 else zr[way, s - 1, q]
            o = jnp.dot(lt[way * 4 + q], block, preferred_element_type=F32) * scale
            rows = o.astype(BF16).reshape(2, 2, 64, 128)
            for p in range(2):
                for hh in range(2):
                    ob[way, s, hh, q, p] = rows[p, hh]
            if 0 < s < 4:
                back = (o[0:128].T.astype(BF16), (-o[128:256]).T.astype(BF16))
                for p in range(2):
                    for hh in range(2):
                        mb[way, s - 1, hh, q, p] = back[p][hh * 64 : (hh + 1) * 64]

        olocal(way, s).start()
        ocopy(way, s).start()
        if 0 < s < 4:
            bcopy(way, s, 0).start()
            bcopy(way, s, 1).start()

    def step(s):
        correlate(0, s)
        correlate(1, s)

    pass_on(1, 1)
    step(0)
    pass_on(0, 0)
    step(1)
    pass_on(3, 2)
    pass_on(2, 1)
    pass_on(1, 0)
    step(2)
    pass_on(3, 1)
    pass_on(2, 0)
    step(3)
    @pl.when(ci < n - 1)
    def _():
        hcopy(0).wait_send()
        hcopy(1).wait_send()

    mcopy.wait_send()

    @pl.loop(1, 2 * n)
    def _(e):
        for fb in range(3):
            xcopy(fb, e).wait_send()

    pass_on(3, 0)
    step(4)


    for way in range(2):
        for s in range(4):
            for fb in range(3):
                zcopy(way, s, fb).wait_send()
        for s in range(5):
            olocal(way, s).wait()
            ocopy(way, s).wait_send()
            ocopy(way, s).wait_recv()
        for s in range(1, 4):
            for hh in range(2):
                bcopy(way, s, hh).wait_send()
                pltpu.make_async_remote_copy(
                    mb.at[way, s - 1, hh], o_ref.at[home(way), :, :, lanes(0)],
                    bsend.at[way, s - 1, hh], brecv.at[way, s - 1, hh],
                    device_id={"chan": ci, "stn": at(shift(way, s), hh)}, device_id_type=MESH,
                ).wait_recv()


def shards(voltages, pfb_taps, flags):
    n = lax.axis_size("stn")
    table = jnp.asarray(dft_table(pfb_taps.shape[1]))
    hot = jnp.asarray(spread(flags.shape[0], 3, 128))
    vm = pl.BlockSpec(memory_space=pltpu.VMEM)
    anywhere = pl.BlockSpec(memory_space=pl.ANY)
    dma = pltpu.SemaphoreType.DMA
    rows = pl.pallas_call(
        functools.partial(kernel, n),
        out_shape=pltpu.VMEM((n, 2, 64, 1024), BF16),
        in_specs=[anywhere] * 5,
        out_specs=vm,
        scratch_shapes=[
            pltpu.VMEM(pfb_taps.shape, F32),
            pltpu.VMEM(table.shape, BF16),
            pltpu.VMEM(flags.shape, jnp.int32),
            pltpu.VMEM(hot.shape, BF16),
            pltpu.VMEM((48, flags.shape[0]), F32),
            pltpu.VMEM((2, n // 2, n, 3 * flags.shape[0]), BF16),
            pltpu.VMEM((64, 39 * 512), BF16),
            pltpu.VMEM((512, 512), BF16),
            pltpu.VMEM((2048, 128), F32),
            pltpu.VMEM((3, n, 2, n // 2, 8, 128), BF16),
            pltpu.VMEM((3, 2, n, n // 2, 8, 128), BF16),
            pltpu.VMEM((2, n // 2, n, 3 * flags.shape[0]), BF16),
            pltpu.VMEM((3, n * n, 128), F32),
            pltpu.VMEM((8, 768, 128), BF16),
            pltpu.VMEM((8, 256, 768), BF16),
            pltpu.VMEM((2, 4, 4, 768, 128), BF16),
            pltpu.VMEM((2, 5, 2, 4, 2, 64, 128), BF16),
            pltpu.VMEM((2, 3, 2, 4, 2, 64, 128), BF16),
            dma, dma((2,)), dma((2,)), dma, dma, dma((3, 2 * n)), dma((3, 2 * n)),
            dma((2, 4, 3)), dma((2, 4, 3)), dma((2, 5)), dma((2, 5)),
            dma((2, 3, 2)), dma((2, 3, 2)), dma((4,)), dma((2, 5)), dma((4,)),
        ],
        compiler_params=pltpu.CompilerParams(
            collective_id=0, has_side_effects=True, vmem_limit_bytes=56 << 20
        ),
        name="correlate",
    )(voltages, pfb_taps, table, flags, hot)
    return rows.astype(F32)


def solution(mesh):
    placed = (P("stn", "chan"), P(), P("stn", "chan", None))
    return jax.shard_map(
        shards, mesh=mesh, in_specs=placed, out_specs=P("chan", None, "stn", None), check_vma=False
    )
```

```python
import functools
import math

import jax
import jax.numpy as jnp
import ml_dtypes
import numpy as np
from jax import lax
from jax.experimental import pallas as pl
from jax.experimental.pallas import tpu as pltpu
from jax.sharding import PartitionSpec as P

POLS = 2
BF16 = jnp.bfloat16
F32 = jnp.float32
MESH = pl.DeviceIdType.MESH


def dft_table(length):
    sample = np.arange(length)
    phase = (np.arange(length // 2)[:, None] * sample[None, :]) % length
    angles = (phase.astype(np.float32) * np.float32(2.0 * math.pi / length)).astype(np.float64)
    values = np.concatenate([np.cos(angles), -np.sin(angles)], axis=0)
    return (values.astype(np.float32) / np.float32(math.sqrt(length))).astype(ml_dtypes.bfloat16)


def spread(stations, blocks, lanes):
    out = np.zeros((blocks, blocks * stations, lanes), np.float32)
    for fb in range(blocks):
        for lane in range(lanes):
            out[fb, fb * stations + (lane % (lanes // 2)) // POLS, lane] = 1.0
    return out.astype(ml_dtypes.bfloat16)


def kernel(
    n,
    v_ref, taps_in, tab_in, flags_in, spread_in,
    o_ref,
    early, taps_ref, tab_ref, flags_ref, spread_ref, fcol, mask_ref, ext, filt, w32, wb, rx, mk, mx, zo, lt, zr, ob, mb,
    vsem, hsend, hrecv, msend, mrecv, xsend, xrecv, zsend, zrecv, osend, orecv, bsend, brecv, lsem, olsem, isem,
):
    ci = lax.axis_index("chan")
    sk = lax.axis_index("stn")
    nfft = 512
    halo = 15
    own = v_ref.shape[1] // nfft
    planes = n // 2
    z = sk // 2
    h = lax.rem(sk, 2)

    def at(dz, hh):
        return lax.rem(z + dz + planes, planes) * 2 + hh

    bar = pltpu.get_barrier_semaphore()

    def greet(chan, stn):
        pl.semaphore_signal(bar, inc=1, device_id={"chan": chan, "stn": stn}, device_id_type=MESH)

    @pl.loop(0, 2)
    def _(hh):
        for dz in (3, -3, 2, -2, 1, -1):
            greet(ci, at(dz, hh))

    @pl.loop(1, 2 * n)
    def _(e):
        greet(lax.rem(ci + e // 2, n), z * 2 + lax.rem(h + e, 2))

    load = pltpu.make_async_copy(v_ref, ext.at[:, halo * nfft :], vsem)
    load.start()
    flags_load = pltpu.make_async_copy(flags_in, flags_ref, isem.at[0])
    taps_load = pltpu.make_async_copy(taps_in, taps_ref, isem.at[1])
    tab_load = pltpu.make_async_copy(tab_in, tab_ref, isem.at[2])
    spread_load = pltpu.make_async_copy(spread_in, spread_ref, isem.at[3])
    for each in (flags_load, taps_load, tab_load, spread_load):
        each.start()

    def fir(fb):
        @pl.loop(0, 16)
        def _(idx):
            s0 = pl.multiple_of((idx // 4) * 16, 16)
            n0 = pl.multiple_of(lax.rem(idx, 4) * 128, 128)
            taps = [taps_ref[pl.ds(k, 1), pl.ds(n0, 128)] for k in range(16)]
            x = [
                ext[pl.ds(s0, 16), pl.ds(pl.multiple_of((fb * 8 + f) * nfft + n0, 128), 128)].astype(F32)
                for f in range(23)
            ]
            for t in range(8):
                acc = taps[0] * x[t + 15]
                for k in range(1, 16):
                    acc = acc + taps[k] * x[t + 15 - k]
                filt[pl.ds(pl.multiple_of(t * 64 + s0, 16), 16), pl.ds(n0, 128)] = acc.astype(BF16)

    def dft(fb):
        for tt in range(2):
            for p in range(2):
                o = lax.dot_general(
                    tab_ref[p * 256 : (p + 1) * 256, :], filt[tt * 256 : (tt + 1) * 256, :],
                    (((1,), (1,)), ((), ())), preferred_element_type=F32,
                )
                for half in range(2):
                    w32[pl.ds(p * 4 + tt * 2 + half, 256, stride=8), :] = o[:, half * 128 : (half + 1) * 128]

        @pl.loop(0, n)
        def _(i):
            rows = w32[pl.ds(pl.multiple_of(i * 128, 128), 128), :]
            wb[fb, i] = rows.reshape(2, n // 2, 8, 128).astype(BF16)

    def xcopy(fb, e):
        chan = lax.rem(ci + e // 2, n)
        hh = lax.rem(h + e, 2)
        return pltpu.make_async_remote_copy(
            wb.at[fb, chan, hh], rx.at[fb, h, ci], xsend.at[fb, e], xrecv.at[fb, e],
            device_id={"chan": chan, "stn": z * 2 + hh}, device_id_type=MESH,
        )

    def xlocal(fb):
        return pltpu.make_async_copy(wb.at[fb, ci, h], rx.at[fb, h, ci], lsem.at[fb])

    mcopy = pltpu.make_async_remote_copy(
        mask_ref.at[1 - h], mk.at[h], msend, mrecv,
        device_id={"chan": ci, "stn": z * 2 + 1 - h}, device_id_type=MESH,
    )
    mlocal = pltpu.make_async_copy(mask_ref.at[h], mk.at[h], lsem.at[3])

    def hcopy(part):
        first, count = ((8, 7), (0, 8))[part]
        return pltpu.make_async_remote_copy(
            v_ref.at[:, pl.ds((own - halo + first) * nfft, count * nfft)],
            ext.at[:, pl.ds(first * nfft, count * nfft)],
            hsend.at[part], hrecv.at[part],
            device_id={"chan": lax.rem(ci + 1, n), "stn": sk}, device_id_type=MESH,
        )

    def xstart(fb):
        xlocal(fb).start()

        @pl.loop(1, 2 * n)
        def _(e):
            xcopy(fb, e).start()

    def halo_wait(part):
        first, count = ((8, 7), (0, 8))[part]

        @pl.when(ci > 0)
        def _():
            hcopy(part).wait_recv()

        @pl.when(ci == 0)
        def _():
            ext[:, first * nfft : (first + count) * nfft] = jnp.zeros((64, count * nfft), BF16)

    lane = lax.broadcasted_iota(jnp.int32, (128, 128), 1)
    low = lane < 64
    row = lax.broadcasted_iota(jnp.int32, (n, 8, 128), 1)

    def zcopy(way, s, fb):
        src = zo.at[pl.ds(way * 4, 4)] if s == 0 else zr.at[way, s - 1]
        part = pl.ds(fb * 256, 256)
        return pltpu.make_async_remote_copy(
            src.at[:, part, :], zr.at[way, s, :, part, :], zsend.at[way, s, fb], zrecv.at[way, s, fb],
            device_id={"chan": ci, "stn": at(1 - 2 * way, h)}, device_id_type=MESH,
        )

    def assemble(fb):
        xlocal(fb).wait()

        @pl.loop(1, 2 * n)
        def _(e):
            xcopy(fb, e).wait_recv()

        @pl.loop(0, 8)
        def _(q):
            both = []
            for hh in range(2):
                data = rx[fb, hh, :, q].astype(F32)
                flag = mx[fb, pl.ds(pl.multiple_of((hh * 8 + q) * n, n), n), :]
                both.append((data * flag.reshape(n, 1, 128)).reshape(128, 128))
            turned = [pltpu.roll(b, 64, 1) for b in both]
            zo[q, fb * 256 : fb * 256 + 128, :] = jnp.where(low, both[0], turned[1]).astype(BF16)
            zo[q, fb * 256 + 128 : fb * 256 + 256, :] = jnp.where(low, turned[0], both[1]).astype(BF16)

        for way in range(2):
            zcopy(way, 0, fb).start()

    def turn(fb):
        @pl.loop(0, 8)
        def _(q):
            for part in range(2):
                r0 = fb * 256 + part * 128
                b = zo[q, r0 : r0 + 128, :].astype(F32)
                y = pltpu.roll(b.reshape(n, 8, 128), 4, 1)
                y = jnp.where(row < 4, y, -y).reshape(128, 128)
                lt[q, 0:128, r0 : r0 + 128] = b.T.astype(BF16)
                lt[q, 128:256, r0 : r0 + 128] = y.T.astype(BF16)

    flags_load.wait()
    stations = flags_ref.shape[0]
    for c in range(n):
        fcol[...] = flags_ref[:, c, :].astype(F32).T
        for fb in range(3):
            mask_ref[c // (n // 2), c % (n // 2), :, fb * stations : (fb + 1) * stations] = fcol[
                pl.ds(fb, n, stride=3), :
            ].astype(BF16)

    load.wait()
    taps_load.wait()
    fir(2)
    tab_load.wait()
    spread_load.wait()
    dft(2)
    pl.semaphore_wait(bar, 2 * n - 1 + 12)

    mlocal.start()
    mcopy.start()
    xstart(2)

    @pl.when(ci < n - 1)
    def _():
        hcopy(0).start()
        hcopy(1).start()

    mlocal.wait()
    mcopy.wait_recv()
    for fb in range(3):
        mx[fb] = jnp.dot(mk[...].reshape(n * n, mk.shape[3]), spread_ref[fb], preferred_element_type=F32)

    def pass_on(s, fb):
        for way in range(2):
            zcopy(way, s, fb).wait_recv()
            if s < 3:
                zcopy(way, s + 1, fb).start()

    assemble(2)
    halo_wait(0)
    fir(1)
    dft(1)
    xstart(1)
    pass_on(0, 2)
    halo_wait(1)
    fir(0)
    dft(0)
    xstart(0)
    turn(2)
    pass_on(1, 2)
    assemble(1)
    turn(1)
    pass_on(0, 1)
    pass_on(2, 2)
    assemble(0)
    turn(0)

    scale = 1.0 / (own * n)

    def home(way):
        return pl.ds(h * 8 + way * 4, 4)

    def lanes(dz):
        return pl.ds(pl.multiple_of(lax.rem(z + dz + planes, planes) * 128, 128), 128)

    def shift(way, s):
        return s if way == 1 else -s

    def olocal(way, s):
        return pltpu.make_async_copy(
            ob.at[way, s, h], o_ref.at[home(way), :, :, lanes(shift(way, s))], olsem.at[way, s]
        )

    def ocopy(way, s):
        return pltpu.make_async_remote_copy(
            ob.at[way, s, 1 - h], o_ref.at[home(way), :, :, lanes(shift(way, s))],
            osend.at[way, s], orecv.at[way, s],
            device_id={"chan": ci, "stn": z * 2 + 1 - h}, device_id_type=MESH,
        )

    def bcopy(way, s, hh):
        return pltpu.make_async_remote_copy(
            mb.at[way, s - 1, hh], o_ref.at[home(way), :, :, lanes(0)],
            bsend.at[way, s - 1, hh], brecv.at[way, s - 1, h],
            device_id={"chan": ci, "stn": at(shift(way, s), hh)}, device_id_type=MESH,
        )

    def correlate(way, s):
        @pl.loop(0, 4)
        def _(q):
            block = zo[way * 4 + q] if s == 0 else zr[way, s - 1, q]
            if s == 4:
                o = jnp.dot(lt[way * 4 + q, :, 0:256], block[0:256], preferred_element_type=F32)
                o = (o + early[way, q]) * scale
            else:
                o = jnp.dot(lt[way * 4 + q], block, preferred_element_type=F32) * scale
            rows = o.astype(BF16).reshape(2, 2, 64, 128)
            for p in range(2):
                for hh in range(2):
                    ob[way, s, hh, q, p] = rows[p, hh]
            if 0 < s < 4:
                back = (o[0:128].T.astype(BF16), (-o[128:256]).T.astype(BF16))
                for p in range(2):
                    for hh in range(2):
                        mb[way, s - 1, hh, q, p] = back[p][hh * 64 : (hh + 1) * 64]

        olocal(way, s).start()
        ocopy(way, s).start()
        if 0 < s < 4:
            bcopy(way, s, 0).start()
            bcopy(way, s, 1).start()

    def step(s):
        correlate(0, s)
        correlate(1, s)

    pass_on(1, 1)
    step(0)
    pass_on(0, 0)
    step(1)
    pass_on(3, 2)
    pass_on(2, 1)
    pass_on(1, 0)
    step(2)
    pass_on(3, 1)
    pass_on(2, 0)
    step(3)
    @pl.when(ci < n - 1)
    def _():
        hcopy(0).wait_send()
        hcopy(1).wait_send()

    mcopy.wait_send()

    @pl.loop(1, 2 * n)
    def _(e):
        for fb in range(3):
            xcopy(fb, e).wait_send()

    for way in range(2):

        @pl.loop(0, 4)
        def _(q):
            early[way, q] = jnp.dot(
                lt[way * 4 + q, :, 256:768], zr[way, 3, q, 256:768, :], preferred_element_type=F32
            )

    pass_on(3, 0)
    step(4)


    for way in range(2):
        for s in range(4):
            for fb in range(3):
                zcopy(way, s, fb).wait_send()
        for s in range(5):
            olocal(way, s).wait()
            ocopy(way, s).wait_send()
            ocopy(way, s).wait_recv()
        for s in range(1, 4):
            for hh in range(2):
                bcopy(way, s, hh).wait_send()
                pltpu.make_async_remote_copy(
                    mb.at[way, s - 1, hh], o_ref.at[home(way), :, :, lanes(0)],
                    bsend.at[way, s - 1, hh], brecv.at[way, s - 1, hh],
                    device_id={"chan": ci, "stn": at(shift(way, s), hh)}, device_id_type=MESH,
                ).wait_recv()


def shards(voltages, pfb_taps, flags):
    n = lax.axis_size("stn")
    table = jnp.asarray(dft_table(pfb_taps.shape[1]))
    hot = jnp.asarray(spread(flags.shape[0], 3, 128))
    vm = pl.BlockSpec(memory_space=pltpu.VMEM)
    anywhere = pl.BlockSpec(memory_space=pl.ANY)
    dma = pltpu.SemaphoreType.DMA
    rows = pl.pallas_call(
        functools.partial(kernel, n),
        out_shape=pltpu.VMEM((n, 2, 64, 1024), BF16),
        in_specs=[anywhere] * 5,
        out_specs=vm,
        scratch_shapes=[
            pltpu.VMEM((2, 4, 256, 128), F32),
            pltpu.VMEM(pfb_taps.shape, F32),
            pltpu.VMEM(table.shape, BF16),
            pltpu.VMEM(flags.shape, jnp.int32),
            pltpu.VMEM(hot.shape, BF16),
            pltpu.VMEM((48, flags.shape[0]), F32),
            pltpu.VMEM((2, n // 2, n, 3 * flags.shape[0]), BF16),
            pltpu.VMEM((64, 39 * 512), BF16),
            pltpu.VMEM((512, 512), BF16),
            pltpu.VMEM((2048, 128), F32),
            pltpu.VMEM((3, n, 2, n // 2, 8, 128), BF16),
            pltpu.VMEM((3, 2, n, n // 2, 8, 128), BF16),
            pltpu.VMEM((2, n // 2, n, 3 * flags.shape[0]), BF16),
            pltpu.VMEM((3, n * n, 128), F32),
            pltpu.VMEM((8, 768, 128), BF16),
            pltpu.VMEM((8, 256, 768), BF16),
            pltpu.VMEM((2, 4, 4, 768, 128), BF16),
            pltpu.VMEM((2, 5, 2, 4, 2, 64, 128), BF16),
            pltpu.VMEM((2, 3, 2, 4, 2, 64, 128), BF16),
            dma, dma((2,)), dma((2,)), dma, dma, dma((3, 2 * n)), dma((3, 2 * n)),
            dma((2, 4, 3)), dma((2, 4, 3)), dma((2, 5)), dma((2, 5)),
            dma((2, 3, 2)), dma((2, 3, 2)), dma((4,)), dma((2, 5)), dma((4,)),
        ],
        compiler_params=pltpu.CompilerParams(
            collective_id=0, has_side_effects=True, vmem_limit_bytes=56 << 20
        ),
        name="correlate",
    )(voltages, pfb_taps, table, flags, hot)
    return rows.astype(F32)


def solution(mesh):
    placed = (P("stn", "chan"), P(), P("stn", "chan", None))
    return jax.shard_map(
        shards, mesh=mesh, in_specs=placed, out_specs=P("chan", None, "stn", None), check_vma=False
    )
```
